32 devices in a mesh: wall: 16 (over z, y, x), stream: 2 (over core).
Axes of the slice: x: 2, y: 2, z: 4, core: 2. Of those that a mesh axis runs over, the one named last changes fastest.
Arguments:
- fields: float32 [5, 2, 3072, 2048], P(None, None, 'wall', 'stream'), may hold values from -5 to 5
- wall_velocity: float32 [2, 3072, 2048], P(None, 'wall', 'stream'), may hold values from -6 to 6
- diffusion: float32 [5], replicated, may hold values from 0.5 to 16
Outputs:
- tendency: float32 [5, 2, 3072, 2048], P(None, None, 'wall', 'stream')
- advanced: float32 [5, 2, 3072, 2048], P(None, None, 'wall', 'stream')
The draws below stay inside these ranges and needn't reach their ends.
All inputs are finite; a program needn't handle non-finite values.
Results may differ from the reference program's by a relative error of at most 0.000094.
Values sent between devices are 32-bit elements; how exact they have to be, the bound alone decides.
A program may use at most 128 MiB of HBM per device.

```python
import math
import jax
import jax.numpy as jnp
from jax import lax

FIELDS = 5
Z = 2
NX = 2048
NY = 3072


def draw_fields(key, part):
    first_key = jax.random.fold_in(jax.random.fold_in(key, 11), 0)
    return jnp.clip(jax.random.normal(first_key, (FIELDS, Z, NY, NX), jnp.float32), -5.0, 5.0)


def level_of(rng, dims, cuts, low, high):
    factor_of, own = 1.0, jax.random.fold_in(rng, 6)
    for axis_at, blocks in cuts:
        steps = jnp.exp(jax.random.uniform(jax.random.fold_in(own, axis_at), (blocks,), jnp.float32, low / len(cuts), high / len(cuts)))
        factor_of = factor_of * jnp.repeat(steps, dims[axis_at] // blocks).reshape([-1 if axis == axis_at else 1 for axis in range(len(dims))])
    return factor_of


def noise(rng, extent, spread, most, shards=(), kind=jnp.bfloat16):
    gain = level_of(rng, extent, shards, -0.22, 0.18) if shards else 1.0
    array = jax.random.normal(rng, extent, jnp.float32) * spread * gain
    return jnp.minimum(jnp.maximum(array, -most), most).astype(kind)


def setup_inputs(seed: int = 0) -> dict:
    key_of = jax.random.split(jax.random.key(seed), 4)
    return {
        "fields": draw_fields(jax.random.fold_in(key_of[3], 71), 0),
        "wall_velocity": noise(key_of[1], (Z, NY, NX), 1.0, 6.0, ((1, 16), (2, 2)), jnp.float32),
        "diffusion": jnp.clip(jnp.exp(jax.random.uniform(key_of[2], (FIELDS,), jnp.float32, math.log(0.5), math.log(16.0))), 0.5, 16.0),
    }


compact_alpha = 1.0 / 3.0
compact_near = 14.0 / 9.0
compact_far = 1.0 / 9.0
time_step = 0.25

def banded_solve(band, centre, source):
    planes, height, width = source.shape
    ones = jnp.ones((height,), dtype=source.dtype)
    lower = (band * ones).at[0].set(0.0)
    upper = (band * ones).at[height - 1].set(0.0)
    middle = centre * ones
    stacked = jnp.transpose(source, (1, 0, 2)).reshape(height, planes * width)
    solved = lax.linalg.tridiagonal_solve(lower, middle, upper, stacked)
    return jnp.transpose(solved.reshape(height, planes, width), (1, 0, 2))

def one_field(field, rate, stream_speed, wall_velocity):
    height = field.shape[1]
    streamwise = (45.0 * (jnp.roll(field, -1, 2) - jnp.roll(field, 1, 2)) - 9.0 * (jnp.roll(field, -2, 2) - jnp.roll(field, 2, 2)) + (jnp.roll(field, -3, 2) - jnp.roll(field, 3, 2))) / 60.0
    padded = jnp.pad(field, ((0, 0), (2, 2), (0, 0)))
    source = 0.5 * compact_near * (padded[:, 3:height + 3] - padded[:, 1:height + 1]) + 0.25 * compact_far * (padded[:, 4:height + 4] - padded[:, 0:height])
    unit = jnp.ones((), dtype=field.dtype)
    normal_slope = banded_solve(compact_alpha * unit, unit, source)
    tendency = -(stream_speed * streamwise + wall_velocity * normal_slope)
    smoothed = banded_solve(-rate, 1.0 + 2.0 * rate, 2.0 * field + time_step * tendency)
    return (tendency, smoothed - field)

def reference(fields, wall_velocity, diffusion):
    stream_speed = fields[0]

    def apply_field(pair):
        return one_field(pair[0], pair[1], stream_speed, wall_velocity)
    tendency, advanced = lax.map(apply_field, (fields, diffusion))
    return (tendency, advanced)
```

```python
import functools
import math

import jax
import jax.numpy as jnp
import numpy as np
from jax import lax
from jax.experimental import pallas as pl
from jax.experimental.pallas import tpu as pltpu
from jax.sharding import PartitionSpec as P

MESH = pl.DeviceIdType.MESH
compact_alpha = 1.0 / 3.0
compact_near = 14.0 / 9.0
compact_far = 1.0 / 9.0
time_step = 0.25
lane = 128
sub = 8


def compact_operator(height):
    band = compact_alpha
    a = np.eye(height) + band * (np.eye(height, k=1) + np.eye(height, k=-1))
    wide = np.zeros((height, height + 4))
    for j in range(height):
        wide[j, j + 3] += 0.5 * compact_near
        wide[j, j + 1] -= 0.5 * compact_near
        wide[j, j + 4] += 0.25 * compact_far
        wide[j, j] -= 0.25 * compact_far
    source = np.concatenate(
        [wide[:, 2 : height + 2], wide[:, :2], wide[:, height + 2 :], np.zeros((height, 2))], axis=1
    )
    source[0, height + 4] = -band
    source[height - 1, height + 5] = -band
    return np.linalg.solve(a, source)


def merge_table(gamma, eta, count, me):
    like = gamma + 0.0 * me.astype(jnp.float32)
    ll, lr, rl, rr = 1.0 + 0.0 * like, 0.0 * like, 0.0 * like, 1.0 + 0.0 * like
    rows = []
    bit = 1
    while bit < count:
        right = (me // bit) % 2 == 1
        inv = 1.0 / (1.0 - gamma * gamma)
        near, far = inv * eta, inv * eta * gamma
        add_l = jnp.where(right, ll, lr)
        add_r = jnp.where(right, rl, rr)
        rows.append(jnp.stack([inv, gamma, eta, add_l, add_r]))
        ll, lr = (
            jnp.where(right, ll * near, ll + lr * far),
            jnp.where(right, lr + ll * far, lr * near),
        )
        rl, rr = (
            jnp.where(right, rl * near, rl + rr * far),
            jnp.where(right, rr + rl * far, rr * near),
        )
        gamma, eta = gamma + eta * eta * gamma * inv, eta * eta * inv
        bit *= 2
    return jnp.stack(rows).reshape(-1)


def row_to_tile(dst, row):
    for t in range(row.shape[-1] // lane):
        dst[t : t + 1, :] = row[:, t * lane : (t + 1) * lane]


def partners(count):
    me = lax.axis_index("wall")
    out = []
    bit = 1
    while bit < count:
        out.append((bit, me + bit * (1 - 2 * ((me // bit) % 2))))
        bit *= 2
    return me, out


def exchange(count, nf, table, buf, got, send, recv, xl, xr):
    me, others = partners(count)
    per = buf.shape[2] // nf
    xl[...] = jnp.zeros(xl.shape, jnp.float32)
    xr[...] = jnp.zeros(xr.shape, jnp.float32)
    for s, (bit, other) in enumerate(others):
        copy = pltpu.make_async_remote_copy(
            src_ref=buf.at[s],
            dst_ref=got.at[s],
            send_sem=send.at[s],
            recv_sem=recv.at[s],
            device_id={"wall": other},
            device_id_type=MESH,
        )
        copy.start()
        copy.wait()
        right = (me // bit) % 2 == 1
        for k in range(nf):
            at = pl.ds(k * per, per)
            inv, gamma, eta, add_l, add_r = (table[(s * 5 + c) * nf + k] for c in range(5))
            fo, lo, fp, lp = buf[s, 0, at], buf[s, 1, at], got[s, 0, at], got[s, 1, at]
            f1, l1 = jnp.where(right, fp, fo), jnp.where(right, lp, lo)
            f2, l2 = jnp.where(right, fo, fp), jnp.where(right, lo, lp)
            head = inv * (f2 + gamma * l1)
            tail = inv * (l1 + gamma * f2)
            value = jnp.where(right, tail, head)
            xl[at] += add_l * value
            xr[at] += add_r * value
            if s + 1 < len(others):
                buf[s + 1, 0, at] = f1 + eta * head
                buf[s + 1, 1, at] = l2 + eta * tail


def first_kernel(count, streams, nf, ends, table, coef, fields, bc, strips, planes, edge, halo, sides,
                 got_strip, buf, got, xl, xr, local_sem, hs, hr, ss, sr, send, recv):
    me, others = partners(count)
    np_, height, width = planes.shape
    strip = sides.shape[2]
    tops = pltpu.make_async_copy(fields.at[:, pl.ds(0, sub)], edge.at[0], local_sem.at[np_])
    bots = pltpu.make_async_copy(fields.at[:, pl.ds(height - sub, sub)], edge.at[1], local_sem.at[np_ + 1])
    tops.start()
    bots.start()
    loads = [
        pltpu.make_async_copy(fields.at[p], planes.at[p], local_sem.at[p]) for p in range(np_)
    ]
    for load in loads:
        load.start()
    halo[2:4] = jnp.zeros((2,) + halo.shape[1:], jnp.float32)
    col = lax.axis_index("stream")
    nexts = [lax.rem(col + 1, streams)] if streams == 2 else [
        lax.rem(col + 1, streams), lax.rem(col + streams - 1, streams)]
    has_left, has_right = me > 0, me < count - 1
    barrier = pltpu.get_barrier_semaphore()
    for _, other in others:
        pl.semaphore_signal(barrier, inc=1, device_id={"wall": other}, device_id_type=MESH)
    for other in nexts:
        pl.semaphore_signal(barrier, inc=1, device_id={"stream": other}, device_id_type=MESH)

    @pl.when(has_left)
    def _():
        pl.semaphore_signal(barrier, inc=1, device_id={"wall": me - 1}, device_id_type=MESH)

    @pl.when(has_right)
    def _():
        pl.semaphore_signal(barrier, inc=1, device_id={"wall": me + 1}, device_id_type=MESH)

    tops.wait()
    bots.wait()
    for p in range(np_):
        for r in range(2):
            row_to_tile(halo.at[0, r, p], edge[0, p, r : r + 1, :])
            row_to_tile(halo.at[1, r, p], edge[1, p, sub - 2 + r : sub - 1 + r, :])
    pl.semaphore_wait(
        barrier,
        len(others) + len(nexts) + has_left.astype(jnp.int32) + has_right.astype(jnp.int32),
    )

    to_left = pltpu.make_async_remote_copy(
        src_ref=halo.at[0], dst_ref=halo.at[3], send_sem=hs.at[0], recv_sem=hr.at[0],
        device_id={"wall": me - 1}, device_id_type=MESH)
    to_right = pltpu.make_async_remote_copy(
        src_ref=halo.at[1], dst_ref=halo.at[2], send_sem=hs.at[1], recv_sem=hr.at[1],
        device_id={"wall": me + 1}, device_id_type=MESH)

    @pl.when(has_left)
    def _():
        to_left.start()

    @pl.when(has_right)
    def _():
        to_right.start()

    low = lax.broadcasted_iota(jnp.int32, (height, strip), 1) < strip // 2
    step = 256
    for p in range(np_):
        loads[p].wait()
        sides[p] = jnp.where(low, planes[p, :, :strip], planes[p, :, width - strip :])
        for c in range(0, width, step):
            f = planes[p, :, c : c + step]
            for e in range(2):
                w = coef[e]
                row = jnp.sum(f * jnp.concatenate([w] * (step // lane), axis=1), axis=0, keepdims=True)
                for t in range(step // lane):
                    buf[0, e, p, c // lane + t : c // lane + t + 1, :] = row[:, t * lane : (t + 1) * lane]
    side_copies = [
        pltpu.make_async_remote_copy(
            src_ref=sides, dst_ref=got_strip.at[i], send_sem=ss.at[i], recv_sem=sr.at[i],
            device_id={"stream": other}, device_id_type=MESH)
        for i, other in enumerate(nexts)
    ]
    for copy in side_copies:
        copy.start()

    @pl.when(has_left)
    def _():
        to_left.wait_send()
        to_right.wait_recv()

    @pl.when(has_right)
    def _():
        to_right.wait_send()
        to_left.wait_recv()

    for e in range(2):
        buf[0, e] = (buf[0, e] + ends[e][0] * halo[2, 0] + ends[e][1] * halo[2, 1]
                     + ends[e][2] * halo[3, 0] + ends[e][3] * halo[3, 1])
    exchange(count, nf, table, buf, got, send, recv, xl, xr)
    for r in range(2):
        bc[r] = halo[2, r]
        bc[2 + r] = halo[3, r]
    bc[4] = xl[...]
    bc[5] = xr[...]
    for copy in side_copies:
        copy.wait()
    strips[...] = got_strip[...]


def second_kernel(count, nf, table, q_edges, out, buf, got, xl, xr, send, recv):
    _, others = partners(count)
    barrier = pltpu.get_barrier_semaphore()
    for _, other in others:
        pl.semaphore_signal(barrier, inc=1, device_id={"wall": other}, device_id_type=MESH)
    buf[0] = q_edges[...]
    pl.semaphore_wait(barrier, len(others))
    exchange(count, nf, table, buf, got, send, recv, xl, xr)
    out[0] = xl[...]
    out[1] = xr[...]


def dot3(ah, al, bh, bl):
    one = functools.partial(jnp.dot, preferred_element_type=jnp.float32)
    return one(ah, bh) + (one(al, bh) + one(ah, bl))


def halves(x):
    hi = x.astype(jnp.bfloat16)
    return hi, (x - hi.astype(jnp.float32)).astype(jnp.bfloat16)


def main_kernel(f_ref, u_ref, v_ref, bc_ref, prev_ref, next_ref, m_ref, g_ref, t_ref, a_ref, q_ref,
                pad, rows, fh, fl):
    height, width = f_ref.shape[1], f_ref.shape[2]
    strip = prev_ref.shape[3]
    extra = rows.shape[0]
    mh, ml = halves(m_ref[...])
    gh, gl = halves(g_ref[0])
    pad[:, :strip] = prev_ref[0, 0]
    pad[:, strip + width :] = next_ref[0, 0]
    pad[:, strip : strip + width] = f_ref[0]
    total = width + 2 * strip
    for r in range(0, height, 16):
        x = pad[r : r + 16, :]

        def at(offset):
            return pltpu.roll(x, (total - offset) % total, 1)

        sw = (45.0 * (at(1) - at(-1)) - 9.0 * (at(2) - at(-2)) + (at(3) - at(-3))) * (1.0 / 60.0)
        t_ref[0, r : r + 16, :] = u_ref[0, r : r + 16, :] * sw[:, strip : strip + width]
    rows[...] = jnp.zeros(rows.shape, jnp.float32)
    for i in range(6):
        for t in range(width // lane):
            rows[i : i + 1, t * lane : (t + 1) * lane] = bc_ref[i, 0, t : t + 1, :]
    step = 256
    for c in range(0, width, step):
        cs = slice(c, c + step)
        fh[:height], fl[:height] = halves(f_ref[0, :, cs])
        fh[height:], fl[height:] = halves(rows[:, cs])
        slope = dot3(mh, ml, fh[...], fl[...])
        t = -(t_ref[0, :, cs] + v_ref[0, :, cs] * slope)
        t_ref[0, :, cs] = t
        f = f_ref[0, :, cs]
        rh, rl = halves(2.0 * f + time_step * t)
        q = dot3(gh, gl, rh, rl)
        a_ref[0, :, cs] = q - f
        for t in range(step // lane):
            ts = slice(t * lane, (t + 1) * lane)
            q_ref[0, 0, c // lane + t : c // lane + t + 1, :] = q[:1, ts]
            q_ref[1, 0, c // lane + t : c // lane + t + 1, :] = q[height - 1 :, ts]


def last_kernel(a_ref, x_ref, w_ref, o_ref):
    width = a_ref.shape[2]
    for t in range(width // lane):
        ts = slice(t * lane, (t + 1) * lane)
        o_ref[0, :, ts] = (a_ref[0, :, ts] + w_ref[0, 0] * x_ref[0, 0, t : t + 1, :]
                           + w_ref[0, 1] * x_ref[1, 0, t : t + 1, :])


def on_device(count, streams, fields, wall_velocity, diffusion):
    nf, nz, height, width = fields.shape
    planes = nf * nz
    tiles = width // lane
    f32 = jnp.float32
    steps = int(math.log2(count))
    flat = fields.reshape(planes, height, width)
    me = lax.axis_index("wall")

    operator = compact_operator(height)
    extra = 16
    wide = np.zeros((height, height + extra), np.float32)
    wide[:, : height + 6] = operator
    gamma1 = float(operator[0, height + 4])
    eta1 = float(operator[0, height + 5])
    ends = [[float(operator[j, height + i]) for i in range(4)] for j in (0, height - 1)]
    coef = np.stack([np.repeat(operator[j, :height, None], lane, 1) for j in (0, height - 1)]).astype(np.float32)

    larger = 0.5 * (1.0 + 2.0 * diffusion + jnp.sqrt(1.0 + 4.0 * diffusion))
    base = diffusion / larger
    log = jnp.log(base)[:, None, None]

    def rising(k):
        return 1.0 - jnp.exp(2.0 * k.astype(f32) * log)

    def green(i, j):
        most, least = jnp.maximum(i, j), jnp.minimum(i, j)
        scale = (larger * (1.0 - base * base))[:, None, None] * rising(jnp.full((1, 1), height + 1))
        return jnp.exp((most - least).astype(f32) * log) * rising(least + 1) * rising(height - most) / scale

    ids = jnp.arange(height, dtype=jnp.int32)
    inverse = green(ids[:, None], ids[None, :])
    rate = diffusion[:, None, None]
    weights = rate[:, None] * jnp.stack(
        [green(ids[:, None], jnp.full((1, lane), e)) for e in (0, height - 1)], axis=1)
    corner = diffusion[:, None] * green(jnp.zeros((1, 2), jnp.int32), jnp.array([[0, height - 1]]))[:, 0]
    table1 = merge_table(jnp.full((nf,), gamma1, f32), jnp.full((nf,), eta1, f32), count, me)
    table2 = merge_table(corner[:, 0], corner[:, 1], count, me)

    vmem = pl.BlockSpec(memory_space=pltpu.VMEM)
    smem = pl.BlockSpec(memory_space=pltpu.SMEM)
    hbm = pl.BlockSpec(memory_space=pl.ANY)
    nrecv = 1 if streams == 2 else 2
    line = (planes, tiles, lane)
    dma = pltpu.SemaphoreType.DMA
    bc, strips = pl.pallas_call(
        functools.partial(first_kernel, count, streams, nf, ends),
        out_shape=(
            jax.ShapeDtypeStruct((6,) + line, f32),
            jax.ShapeDtypeStruct((nrecv, planes, height, lane), f32),
        ),
        in_specs=[smem, vmem, hbm],
        out_specs=(vmem, vmem),
        scratch_shapes=[
            pltpu.VMEM((planes, height, width), f32),
            pltpu.VMEM((2, planes, sub, width), f32),
            pltpu.VMEM((4, 2) + line, f32),
            pltpu.VMEM((planes, height, lane), f32),
            pltpu.VMEM((nrecv, planes, height, lane), f32),
            pltpu.VMEM((steps, 2) + line, f32),
            pltpu.VMEM((steps, 2) + line, f32),
            pltpu.VMEM(line, f32),
            pltpu.VMEM(line, f32),
            dma((planes + 2,)), dma((2,)), dma((2,)), dma((nrecv,)), dma((nrecv,)),
            dma((steps,)), dma((steps,)),
        ],
        compiler_params=pltpu.CompilerParams(
            collective_id=0, has_side_effects=True, vmem_limit_bytes=40 * 2**20),
    )(table1, jnp.asarray(coef), flat)

    plane = lambda k, z: k * nz + z
    block = (1, height, width)
    tend, part, q_edges = pl.pallas_call(
        main_kernel,
        grid=(nz, nf),
        out_shape=(
            jax.ShapeDtypeStruct(flat.shape, f32),
            jax.ShapeDtypeStruct(flat.shape, f32),
            jax.ShapeDtypeStruct((2,) + line, f32),
        ),
        in_specs=[
            pl.BlockSpec(block, lambda z, k: (plane(k, z), 0, 0)),
            pl.BlockSpec(block, lambda z, k: (z, 0, 0)),
            pl.BlockSpec(block, lambda z, k: (z, 0, 0)),
            pl.BlockSpec((6, 1, tiles, lane), lambda z, k: (0, plane(k, z), 0, 0)),
            pl.BlockSpec((1, 1, height, lane), lambda z, k: (0, plane(k, z), 0, 0)),
            pl.BlockSpec((1, 1, height, lane), lambda z, k: (nrecv - 1, plane(k, z), 0, 0)),
            pl.BlockSpec((height, height + extra), lambda z, k: (0, 0)),
            pl.BlockSpec((1, height, height), lambda z, k: (k, 0, 0)),
        ],
        out_specs=(
            pl.BlockSpec(block, lambda z, k: (plane(k, z), 0, 0)),
            pl.BlockSpec(block, lambda z, k: (plane(k, z), 0, 0)),
            pl.BlockSpec((2, 1, tiles, lane), lambda z, k: (0, plane(k, z), 0, 0)),
        ),
        scratch_shapes=[
            pltpu.VMEM((height, width + 2 * lane), f32),
            pltpu.VMEM((extra, width), f32),
            pltpu.VMEM((height + extra, 256), jnp.bfloat16),
            pltpu.VMEM((height + extra, 256), jnp.bfloat16),
        ],
        compiler_params=pltpu.CompilerParams(vmem_limit_bytes=40 * 2**20),
    )(flat, flat, wall_velocity, bc, strips, strips, jnp.asarray(wide), inverse)

    beyond = pl.pallas_call(
        functools.partial(second_kernel, count, nf),
        out_shape=jax.ShapeDtypeStruct((2,) + line, f32),
        in_specs=[smem, vmem],
        out_specs=vmem,
        scratch_shapes=[
            pltpu.VMEM((steps, 2) + line, f32),
            pltpu.VMEM((steps, 2) + line, f32),
            pltpu.VMEM(line, f32),
            pltpu.VMEM(line, f32),
            dma((steps,)), dma((steps,)),
        ],
        compiler_params=pltpu.CompilerParams(collective_id=1, has_side_effects=True),
    )(table2, q_edges)

    advanced = pl.pallas_call(
        last_kernel,
        grid=(planes,),
        out_shape=jax.ShapeDtypeStruct(flat.shape, f32),
        in_specs=[
            pl.BlockSpec(block, lambda p: (p, 0, 0)),
            pl.BlockSpec((2, 1, tiles, lane), lambda p: (0, p, 0, 0)),
            pl.BlockSpec((1, 2, height, lane), lambda p: (p // nz, 0, 0, 0)),
        ],
        out_specs=pl.BlockSpec(block, lambda p: (p, 0, 0)),
        input_output_aliases={0: 0},
        compiler_params=pltpu.CompilerParams(vmem_limit_bytes=40 * 2**20),
    )(part, beyond, weights)
    return tend.reshape(fields.shape), advanced.reshape(fields.shape)


def solution(mesh):
    in_specs = (P(None, None, "wall", "stream"), P(None, "wall", "stream"), P())
    out_specs = (P(None, None, "wall", "stream"), P(None, None, "wall", "stream"))
    body = functools.partial(on_device, mesh.shape["wall"], mesh.shape["stream"])
    return jax.shard_map(body, mesh=mesh, in_specs=in_specs, out_specs=out_specs, check_vma=False)
```

```python
import functools
import math

import jax
import jax.numpy as jnp
import numpy as np
from jax import lax
from jax.experimental import pallas as pl
from jax.experimental.pallas import tpu as pltpu
from jax.sharding import PartitionSpec as P

MESH = pl.DeviceIdType.MESH
compact_alpha = 1.0 / 3.0
compact_near = 14.0 / 9.0
compact_far = 1.0 / 9.0
time_step = 0.25
lane = 128
sub = 8


def compact_operator(height):
    band = compact_alpha
    a = np.eye(height) + band * (np.eye(height, k=1) + np.eye(height, k=-1))
    wide = np.zeros((height, height + 4))
    for j in range(height):
        wide[j, j + 3] += 0.5 * compact_near
        wide[j, j + 1] -= 0.5 * compact_near
        wide[j, j + 4] += 0.25 * compact_far
        wide[j, j] -= 0.25 * compact_far
    source = np.concatenate(
        [wide[:, 2 : height + 2], wide[:, :2], wide[:, height + 2 :], np.zeros((height, 2))], axis=1
    )
    source[0, height + 4] = -band
    source[height - 1, height + 5] = -band
    return np.linalg.solve(a, source)


def merge_table(gamma, eta, steps, me):
    one, zero = jnp.ones_like(gamma), jnp.zeros_like(gamma)
    ll, lr, rl, rr = one, zero, zero, one
    rows = []
    for step in range(steps):
        right = (me // 2**step) % 2 == 1
        inv = 1.0 / (1.0 - gamma * gamma)
        near, far = inv * eta, inv * eta * gamma
        rows.append((inv, gamma, eta, jnp.where(right, ll, lr), jnp.where(right, rl, rr)))
        ll, lr = (
            jnp.where(right, ll * near, ll + lr * far),
            jnp.where(right, lr + ll * far, lr * near),
        )
        rl, rr = (
            jnp.where(right, rl * near, rl + rr * far),
            jnp.where(right, rr + rl * far, rr * near),
        )
        gamma, eta = gamma + eta * eta * gamma * inv, eta * eta * inv
    return rows


def diffusive_band(rate):
    larger = 0.5 * (1.0 + 2.0 * rate + jnp.sqrt(1.0 + 4.0 * rate))
    base = rate / larger
    return larger, base, jnp.log(base)


def rising(k, log):
    return 1.0 - jnp.exp(2.0 * k * log)


def edge_weights(rate, ids, height, end):
    larger, base, log = diffusive_band(rate)
    first = ids + 1.0 if end else height - ids
    away = (height - 1.0) - ids if end else ids
    scale = larger * (1.0 - base * base) * rising(height + 1.0, log)
    return rate * jnp.exp(away * log) * rising(first, log) * rising(1.0, log) / scale


def row_to_tile(dst, row):
    for t in range(row.shape[-1] // lane):
        dst[t : t + 1, :] = row[:, t * lane : (t + 1) * lane]


def dot3(ah, al, bh, bl):
    one = functools.partial(jnp.dot, preferred_element_type=jnp.float32)
    return one(ah, bh) + (one(al, bh) + one(ah, bl))


def halves(x):
    hi = x.astype(jnp.bfloat16)
    return hi, (x - hi.astype(jnp.float32)).astype(jnp.bfloat16)


def big_kernel(count, streams, nf, nz, ends, corners, rates, coef, operator, fields, velocity,
               tend, part, beyond,
               planes, wv, edge, halo, sides, strips, buf, got, near, table,
               mh, ml, gh, gl, rows, pad, fh, fl,
               local_sem, wv_sem, hs, hr, ss, sr, send, recv):
    me = lax.axis_index("wall")
    col = lax.axis_index("stream")
    steps = buf.shape[1]
    np_, height, width = planes.shape
    strip = sides.shape[2]
    tiles = width // lane
    tops = pltpu.make_async_copy(fields.at[:, pl.ds(0, sub)], edge.at[0], local_sem.at[np_])
    bots = pltpu.make_async_copy(fields.at[:, pl.ds(height - sub, sub)], edge.at[1], local_sem.at[np_ + 1])
    tops.start()
    bots.start()

    def load(p):
        return pltpu.make_async_copy(fields.at[p], planes.at[p], local_sem.at[p])

    for p in range(np_):
        load(p).start()
    speed = pltpu.make_async_copy(velocity, wv, wv_sem)
    speed.start()
    halo[2:4] = jnp.zeros((2,) + halo.shape[1:], jnp.float32)
    nexts = [lax.rem(col + 1, streams)]
    if streams > 2:
        nexts.append(lax.rem(col + streams - 1, streams))
    has_left, has_right = me > 0, me < count - 1
    others = [me + 2**s * (1 - 2 * ((me // 2**s) % 2)) for s in range(steps)]
    barrier = pltpu.get_barrier_semaphore()
    for other in others:
        pl.semaphore_signal(barrier, inc=1, device_id={"wall": other}, device_id_type=MESH)
    for other in nexts:
        pl.semaphore_signal(barrier, inc=1, device_id={"stream": other}, device_id_type=MESH)

    @pl.when(has_left)
    def _():
        pl.semaphore_signal(barrier, inc=1, device_id={"wall": me - 1}, device_id_type=MESH)

    @pl.when(has_right)
    def _():
        pl.semaphore_signal(barrier, inc=1, device_id={"wall": me + 1}, device_id_type=MESH)

    tops.wait()
    bots.wait()
    for p in range(np_):
        for r in range(2):
            row_to_tile(halo.at[0, r, p], edge[0, p, r : r + 1, :])
            row_to_tile(halo.at[1, r, p], edge[1, p, sub - 2 + r : sub - 1 + r, :])
    pl.semaphore_wait(
        barrier,
        len(others) + len(nexts) + has_left.astype(jnp.int32) + has_right.astype(jnp.int32),
    )
    to_left = pltpu.make_async_remote_copy(
        src_ref=halo.at[0], dst_ref=halo.at[3], send_sem=hs.at[0], recv_sem=hr.at[0],
        device_id={"wall": me - 1}, device_id_type=MESH)
    to_right = pltpu.make_async_remote_copy(
        src_ref=halo.at[1], dst_ref=halo.at[2], send_sem=hs.at[1], recv_sem=hr.at[1],
        device_id={"wall": me + 1}, device_id_type=MESH)

    @pl.when(has_left)
    def _():
        to_left.start()

    @pl.when(has_right)
    def _():
        to_right.start()

    def side(i, p):
        return pltpu.make_async_remote_copy(
            src_ref=sides.at[p], dst_ref=strips.at[i, p], send_sem=ss.at[i, p], recv_sem=sr.at[i, p],
            device_id={"stream": nexts[i]}, device_id_type=MESH)

    low = lax.broadcasted_iota(jnp.int32, (height, strip), 1) < strip // 2

    @pl.loop(0, np_)
    def _(p):
        load(p).wait()
        sides[p] = jnp.where(low, planes[p, :, :strip], planes[p, :, width - strip :])
        for i in range(len(nexts)):
            side(i, p).start()
        field, z = p // nz, p % nz
        for t in range(tiles):
            f = planes[p, :, t * lane : (t + 1) * lane]
            for e in range(2):
                buf[0, 0, field, e, z, t : t + 1, :] = jnp.sum(f * coef[e], axis=0, keepdims=True)

    @pl.when(has_left)
    def _():
        to_left.wait_send()
        to_right.wait_recv()

    @pl.when(has_right)
    def _():
        to_right.wait_send()
        to_left.wait_recv()

    for m, (gamma, eta) in enumerate(corners):
        rows_ = merge_table(jnp.full((tiles, lane), gamma), jnp.full((tiles, lane), eta), steps, me)
        for s in range(steps):
            for c in range(5):
                for k in range(nf):
                    table[m, s, c, k] = rows_[s][c]
    near[...] = jnp.zeros(near.shape, jnp.float32)
    for k in range(nf):
        for e in range(2):
            at = pl.ds(k * nz, nz)
            buf[0, 0, k, e] = (buf[0, 0, k, e]
                               + ends[e][0] * halo[2, 0, at] + ends[e][1] * halo[2, 1, at]
                               + ends[e][2] * halo[3, 0, at] + ends[e][3] * halo[3, 1, at])

    def trade(m, s, k):
        return pltpu.make_async_remote_copy(
            src_ref=buf.at[m, s, k], dst_ref=got.at[m, s, k],
            send_sem=send.at[m, s, k], recv_sem=recv.at[m, s, k],
            device_id={"wall": others[s]}, device_id_type=MESH)

    def merge(m, s, k):
        trade(m, s, k).wait()
        right = (me // 2**s) % 2 == 1
        inv, gamma, eta, add_l, add_r = (table[m, s, c, k] for c in range(5))
        fo, lo, fp, lp = buf[m, s, k, 0], buf[m, s, k, 1], got[m, s, k, 0], got[m, s, k, 1]
        f1, l1 = jnp.where(right, fp, fo), jnp.where(right, lp, lo)
        f2, l2 = jnp.where(right, fo, fp), jnp.where(right, lo, lp)
        ahead = inv * (f2 + gamma * l1)
        behind = inv * (l1 + gamma * f2)
        if s + 1 < steps:
            buf[m, s + 1, k, 0] = f1 + eta * ahead
            buf[m, s + 1, k, 1] = l2 + eta * behind
            trade(m, s + 1, k).start()
        value = jnp.where(right, behind, ahead)
        near[m, k, 0] += add_l * value
        near[m, k, 1] += add_r * value

    @pl.loop(0, nf)
    def _(k):
        trade(0, 0, k).start()

    mh[...], ml[...] = halves(operator[...])
    row = lax.broadcasted_iota(jnp.int32, (height, height), 0).astype(jnp.float32)
    column = lax.broadcasted_iota(jnp.int32, (height, height), 1).astype(jnp.float32)
    down = lax.broadcasted_iota(jnp.int32, (height, 1), 0).astype(jnp.float32)
    along = lax.broadcasted_iota(jnp.int32, (1, height), 1).astype(jnp.float32)

    @pl.loop(0, nf)
    def _(k):
        larger, base, log = diffusive_band(jnp.full((1, height), rates[k], jnp.float32))
        _, _, tall = diffusive_band(jnp.full((height, 1), rates[k], jnp.float32))
        scale = 1.0 / (larger * (1.0 - base * base) * rising(height + 1.0, log))
        upper = rising(down + 1.0, tall) * (rising(height - along, log) * scale)
        lower = rising(height - down, tall) * (rising(along + 1.0, log) * scale)
        green = jnp.exp(jnp.abs(row - column) * log) * jnp.where(row <= column, upper, lower)
        gh[k], gl[k] = halves(green)
        rate = jnp.full((tiles, lane), rates[k], jnp.float32)
        gamma = edge_weights(rate, jnp.zeros((tiles, lane), jnp.float32), height, 0)
        eta = edge_weights(rate, jnp.zeros((tiles, lane), jnp.float32), height, 1)
        for s, cs in enumerate(merge_table(gamma, eta, steps, me)):
            for c in range(5):
                table[1, s, c, k] = cs[c]

    total = width + 2 * strip

    def sweep(p):
        for i in range(len(nexts)):
            side(i, p).wait()
        pad[:, :strip] = strips[0, p]
        pad[:, strip + width :] = strips[len(nexts) - 1, p]
        pad[:, strip : strip + width] = planes[p]
        z = p % nz

        @pl.loop(0, height, step=16)
        def _(r):
            at_rows = pl.ds(pl.multiple_of(r, 16), 16)
            x = pad[at_rows, :]

            def at(offset):
                return pltpu.roll(x, (total - offset) % total, 1)

            sw = (45.0 * (at(1) - at(-1)) - 9.0 * (at(2) - at(-2)) + (at(3) - at(-3))) * (1.0 / 60.0)
            tend[p, at_rows, :] = planes[z, at_rows, :] * sw[:, strip : strip + width]

    for s in range(steps):
        pl.loop(s * np_ // steps, (s + 1) * np_ // steps)(sweep)
        pl.loop(0, nf)(functools.partial(merge, 0, s))
    speed.wait()
    step = 256
    rows[...] = jnp.zeros(rows.shape, jnp.float32)

    def plane(k, z):
        p = k * nz + z
        for t in range(tiles):
            ts = slice(t * lane, (t + 1) * lane)
            for r in range(2):
                rows[r : r + 1, ts] = halo[2, r, p, t : t + 1, :]
                rows[2 + r : 3 + r, ts] = halo[3, r, p, t : t + 1, :]
                rows[4 + r : 5 + r, ts] = near[0, k, r, z, t : t + 1, :]
        for c in range(0, width, step):
            cs = slice(c, c + step)
            f = planes[p, :, cs]
            fh[:height, cs], fl[:height, cs] = halves(f)
            fh[height:, cs], fl[height:, cs] = halves(rows[:, cs])
            slope = dot3(mh[...], ml[...], fh[:, cs], fl[:, cs])
            t_ = -(tend[p, :, cs] + wv[z, :, cs] * slope)
            tend[p, :, cs] = t_
            rh, rl = halves(2.0 * f + time_step * t_)
            q = dot3(gh[k], gl[k], rh, rl)
            part[p, :, cs] = q - f
            for t in range(step // lane):
                ts = slice(t * lane, (t + 1) * lane)
                at_t = slice(c // lane + t, c // lane + t + 1)
                buf[1, 0, k, 0, z, at_t, :] = q[:1, ts]
                buf[1, 0, k, 1, z, at_t, :] = q[height - 1 :, ts]

    @pl.loop(0, nf + steps)
    def _(k):
        @pl.when(k < nf)
        def _():
            pl.loop(0, nz)(functools.partial(plane, k))
            trade(1, 0, k).start()

        for s in range(steps):
            @pl.when(jnp.logical_and(k >= s + 1, k < nf + s + 1))
            def _():
                merge(1, s, k - 1 - s)

    beyond[...] = near[1]


def last_kernel(rates, tend, part, near, t_out, a_out, stage, sem):
    np_, height, width = part.shape
    nf = near.shape[0]
    nz = np_ // nf
    first = pltpu.make_async_copy(tend, t_out, sem.at[np_])
    first.start()
    ids = lax.broadcasted_iota(jnp.int32, (height, lane), 0).astype(jnp.float32)

    def put(p):
        return pltpu.make_async_copy(stage.at[p], a_out.at[p], sem.at[p])

    @pl.loop(0, nf)
    def _(k):
        rate = jnp.full((height, lane), rates[k], jnp.float32)
        wl, wr = (edge_weights(rate, ids, height, e) for e in range(2))
        for z in range(nz):
            p = k * nz + z
            for t in range(width // lane):
                ts = slice(t * lane, (t + 1) * lane)
                stage[p, :, ts] = (part[p, :, ts] + wl * near[k, 0, z, t : t + 1, :]
                                   + wr * near[k, 1, z, t : t + 1, :])
            put(p).start()

    @pl.loop(0, np_)
    def _(p):
        put(p).wait()

    first.wait()


def on_device(count, streams, fields, wall_velocity, diffusion):
    nf, nz, height, width = fields.shape
    planes = nf * nz
    tiles = width // lane
    f32 = jnp.float32
    bf16 = jnp.bfloat16
    steps = int(math.log2(count))
    flat = fields.reshape(planes, height, width)
    operator = compact_operator(height)
    extra = 16
    wide = np.zeros((height, height + extra), np.float32)
    wide[:, : height + 6] = operator
    corners = [(float(operator[0, height + 4]), float(operator[0, height + 5]))]
    ends = [[float(operator[j, height + i]) for i in range(4)] for j in (0, height - 1)]
    coef = np.stack([np.repeat(operator[j, :height, None], lane, 1) for j in (0, height - 1)]).astype(np.float32)

    vmem = pl.BlockSpec(memory_space=pltpu.VMEM)
    smem = pl.BlockSpec(memory_space=pltpu.SMEM)
    hbm = pl.BlockSpec(memory_space=pltpu.HBM)
    nrecv = 1 if streams == 2 else 2
    tile = (tiles, lane)
    dma = pltpu.SemaphoreType.DMA
    whole = jax.ShapeDtypeStruct(flat.shape, f32)
    tend, part, beyond = pl.pallas_call(
        functools.partial(big_kernel, count, streams, nf, nz, ends, corners),
        out_shape=(whole, whole, jax.ShapeDtypeStruct((nf, 2, nz) + tile, f32)),
        in_specs=[smem, vmem, vmem, hbm, hbm],
        out_specs=(vmem, vmem, vmem),
        scratch_shapes=[
            pltpu.VMEM((planes, height, width), f32),
            pltpu.VMEM((nz, height, width), f32),
            pltpu.VMEM((2, planes, sub, width), f32),
            pltpu.VMEM((4, 2, planes) + tile, f32),
            pltpu.VMEM((planes, height, lane), f32),
            pltpu.VMEM((nrecv, planes, height, lane), f32),
            pltpu.VMEM((2, steps, nf, 2, nz) + tile, f32),
            pltpu.VMEM((2, steps, nf, 2, nz) + tile, f32),
            pltpu.VMEM((2, nf, 2, nz) + tile, f32),
            pltpu.VMEM((2, steps, 5, nf) + tile, f32),
            pltpu.VMEM((height, height + extra), bf16),
            pltpu.VMEM((height, height + extra), bf16),
            pltpu.VMEM((nf, height, height), bf16),
            pltpu.VMEM((nf, height, height), bf16),
            pltpu.VMEM((extra, width), f32),
            pltpu.VMEM((height, width + 2 * lane), f32),
            pltpu.VMEM((height + extra, width), bf16),
            pltpu.VMEM((height + extra, width), bf16),
            dma((planes + 2,)), dma, dma((2,)), dma((2,)),
            dma((nrecv, planes)), dma((nrecv, planes)),
            dma((2, steps, nf)), dma((2, steps, nf)),
        ],
        compiler_params=pltpu.CompilerParams(
            collective_id=0, has_side_effects=True, vmem_limit_bytes=36 * 2**20),
    )(diffusion, jnp.asarray(coef), jnp.asarray(wide), flat, wall_velocity)

    tendency, advanced = pl.pallas_call(
        last_kernel,
        out_shape=(whole, whole),
        in_specs=[smem, vmem, vmem, vmem],
        out_specs=(hbm, hbm),
        scratch_shapes=[pltpu.VMEM(flat.shape, f32), dma((planes + 1,))],
        compiler_params=pltpu.CompilerParams(vmem_limit_bytes=16 * 2**20),
    )(diffusion, tend, part, beyond)
    return tendency.reshape(fields.shape), advanced.reshape(fields.shape)


def solution(mesh):
    in_specs = (P(None, None, "wall", "stream"), P(None, "wall", "stream"), P())
    out_specs = (P(None, None, "wall", "stream"), P(None, None, "wall", "stream"))
    body = functools.partial(on_device, mesh.shape["wall"], mesh.shape["stream"])
    return jax.shard_map(body, mesh=mesh, in_specs=in_specs, out_specs=out_specs, check_vma=False)
```

```python
import functools
import math

import jax
import jax.numpy as jnp
import numpy as np
from jax import lax
from jax.experimental import pallas as pl
from jax.experimental.pallas import tpu as pltpu
from jax.sharding import PartitionSpec as P

MESH = pl.DeviceIdType.MESH
compact_alpha = 1.0 / 3.0
compact_near = 14.0 / 9.0
compact_far = 1.0 / 9.0
time_step = 0.25
lane = 128
sub = 8


def compact_operator(height):
    band = compact_alpha
    a = np.eye(height) + band * (np.eye(height, k=1) + np.eye(height, k=-1))
    wide = np.zeros((height, height + 4))
    for j in range(height):
        wide[j, j + 3] += 0.5 * compact_near
        wide[j, j + 1] -= 0.5 * compact_near
        wide[j, j + 4] += 0.25 * compact_far
        wide[j, j] -= 0.25 * compact_far
    source = np.concatenate(
        [wide[:, 2 : height + 2], wide[:, :2], wide[:, height + 2 :], np.zeros((height, 2))], axis=1
    )
    source[0, height + 4] = -band
    source[height - 1, height + 5] = -band
    return np.linalg.solve(a, source)


def merge_table(gamma, eta, steps, me):
    one, zero = jnp.ones_like(gamma), jnp.zeros_like(gamma)
    ll, lr, rl, rr = one, zero, zero, one
    rows = []
    for step in range(steps):
        right = (me // 2**step) % 2 == 1
        inv = 1.0 / (1.0 - gamma * gamma)
        near, far = inv * eta, inv * eta * gamma
        rows.append((inv, gamma, eta, jnp.where(right, ll, lr), jnp.where(right, rl, rr)))
        ll, lr = (
            jnp.where(right, ll * near, ll + lr * far),
            jnp.where(right, lr + ll * far, lr * near),
        )
        rl, rr = (
            jnp.where(right, rl * near, rl + rr * far),
            jnp.where(right, rr + rl * far, rr * near),
        )
        gamma, eta = gamma + eta * eta * gamma * inv, eta * eta * inv
    return rows


def diffusive_band(rate):
    larger = 0.5 * (1.0 + 2.0 * rate + jnp.sqrt(1.0 + 4.0 * rate))
    base = rate / larger
    return larger, base, jnp.log(base)


def rising(k, log):
    return 1.0 - jnp.exp(2.0 * k * log)


def edge_weights(rate, ids, height, end):
    larger, base, log = diffusive_band(rate)
    first = ids + 1.0 if end else height - ids
    away = (height - 1.0) - ids if end else ids
    scale = larger * (1.0 - base * base) * rising(height + 1.0, log)
    return rate * jnp.exp(away * log) * rising(first, log) * rising(1.0, log) / scale


def row_to_tile(dst, row):
    for t in range(row.shape[-1] // lane):
        dst[t : t + 1, :] = row[:, t * lane : (t + 1) * lane]


def dot3(ah, al, bh, bl):
    one = functools.partial(jnp.dot, preferred_element_type=jnp.float32)
    return one(ah, bh) + (one(al, bh) + one(ah, bl))


def halves(x):
    hi = x.astype(jnp.bfloat16)
    return hi, (x - hi.astype(jnp.float32)).astype(jnp.bfloat16)


def big_kernel(count, streams, nf, nz, ends, corners, rates, coef_in, operator_in, fields, velocity,
               tend, part, beyond,
               coef, operator, planes, wv, edge, halo, sides, strips, buf, got, near, table,
               mh, ml, gh, gl, rows, ph, pq, stencil, fh, fl,
               const_sem, local_sem, wv_sem, hs, hr, ss, sr, send, recv):
    me = lax.axis_index("wall")
    col = lax.axis_index("stream")
    steps = buf.shape[1]
    np_, height, width = planes.shape
    strip = sides.shape[2]
    tiles = width // lane
    tops = pltpu.make_async_copy(fields.at[:, pl.ds(0, sub)], edge.at[0], local_sem.at[np_])
    bots = pltpu.make_async_copy(fields.at[:, pl.ds(height - sub, sub)], edge.at[1], local_sem.at[np_ + 1])
    tops.start()
    bots.start()
    consts = [
        pltpu.make_async_copy(coef_in, coef, const_sem.at[0]),
        pltpu.make_async_copy(operator_in, operator, const_sem.at[1]),
    ]
    for const in consts:
        const.start()

    def load(p):
        return pltpu.make_async_copy(fields.at[p], planes.at[p], local_sem.at[p])

    for p in range(np_):
        load(p).start()
    speed = pltpu.make_async_copy(velocity, wv, wv_sem)
    speed.start()
    halo[2:4] = jnp.zeros((2,) + halo.shape[1:], jnp.float32)
    nexts = [lax.rem(col + 1, streams)]
    if streams > 2:
        nexts.append(lax.rem(col + streams - 1, streams))
    has_left, has_right = me > 0, me < count - 1
    others = [me + 2**s * (1 - 2 * ((me // 2**s) % 2)) for s in range(steps)]
    barrier = pltpu.get_barrier_semaphore()
    for other in others:
        pl.semaphore_signal(barrier, inc=1, device_id={"wall": other}, device_id_type=MESH)
    for other in nexts:
        pl.semaphore_signal(barrier, inc=1, device_id={"stream": other}, device_id_type=MESH)

    @pl.when(has_left)
    def _():
        pl.semaphore_signal(barrier, inc=1, device_id={"wall": me - 1}, device_id_type=MESH)

    @pl.when(has_right)
    def _():
        pl.semaphore_signal(barrier, inc=1, device_id={"wall": me + 1}, device_id_type=MESH)

    tops.wait()
    bots.wait()
    for p in range(np_):
        for r in range(2):
            row_to_tile(halo.at[0, r, p], edge[0, p, r : r + 1, :])
            row_to_tile(halo.at[1, r, p], edge[1, p, sub - 2 + r : sub - 1 + r, :])
    pl.semaphore_wait(
        barrier,
        len(others) + len(nexts) + has_left.astype(jnp.int32) + has_right.astype(jnp.int32),
    )
    to_left = pltpu.make_async_remote_copy(
        src_ref=halo.at[0], dst_ref=halo.at[3], send_sem=hs.at[0], recv_sem=hr.at[0],
        device_id={"wall": me - 1}, device_id_type=MESH)
    to_right = pltpu.make_async_remote_copy(
        src_ref=halo.at[1], dst_ref=halo.at[2], send_sem=hs.at[1], recv_sem=hr.at[1],
        device_id={"wall": me + 1}, device_id_type=MESH)

    @pl.when(has_left)
    def _():
        to_left.start()

    @pl.when(has_right)
    def _():
        to_right.start()

    def side(i, p):
        return pltpu.make_async_remote_copy(
            src_ref=sides.at[p], dst_ref=strips.at[i, p], send_sem=ss.at[i, p], recv_sem=sr.at[i, p],
            device_id={"stream": nexts[i]}, device_id_type=MESH)

    for const in consts:
        const.wait()
    low = lax.broadcasted_iota(jnp.int32, (height, strip), 1) < strip // 2

    @pl.loop(0, np_)
    def _(p):
        load(p).wait()
        sides[p] = jnp.where(low, planes[p, :, :strip], planes[p, :, width - strip :])
        for i in range(len(nexts)):
            side(i, p).start()
        field, z = p // nz, p % nz
        for t in range(tiles):
            f = planes[p, :, t * lane : (t + 1) * lane]
            for e in range(2):
                buf[0, 0, field, e, z, t : t + 1, :] = jnp.sum(f * coef[e], axis=0, keepdims=True)

    @pl.when(has_left)
    def _():
        to_left.wait_send()
        to_right.wait_recv()

    @pl.when(has_right)
    def _():
        to_right.wait_send()
        to_left.wait_recv()

    for m, (gamma, eta) in enumerate(corners):
        rows_ = merge_table(jnp.full((tiles, lane), gamma), jnp.full((tiles, lane), eta), steps, me)
        for s in range(steps):
            for c in range(5):
                for k in range(nf):
                    table[m, s, c, k] = rows_[s][c]
    near[...] = jnp.zeros(near.shape, jnp.float32)
    for k in range(nf):
        for e in range(2):
            at = pl.ds(k * nz, nz)
            buf[0, 0, k, e] = (buf[0, 0, k, e]
                               + ends[e][0] * halo[2, 0, at] + ends[e][1] * halo[2, 1, at]
                               + ends[e][2] * halo[3, 0, at] + ends[e][3] * halo[3, 1, at])

    def trade(m, s, k):
        return pltpu.make_async_remote_copy(
            src_ref=buf.at[m, s, k], dst_ref=got.at[m, s, k],
            send_sem=send.at[m, s, k], recv_sem=recv.at[m, s, k],
            device_id={"wall": others[s]}, device_id_type=MESH)

    def merge(m, s, k):
        trade(m, s, k).wait()
        right = (me // 2**s) % 2 == 1
        inv, gamma, eta, add_l, add_r = (table[m, s, c, k] for c in range(5))
        fo, lo, fp, lp = buf[m, s, k, 0], buf[m, s, k, 1], got[m, s, k, 0], got[m, s, k, 1]
        f1, l1 = jnp.where(right, fp, fo), jnp.where(right, lp, lo)
        f2, l2 = jnp.where(right, fo, fp), jnp.where(right, lo, lp)
        ahead = inv * (f2 + gamma * l1)
        behind = inv * (l1 + gamma * f2)
        if s + 1 < steps:
            buf[m, s + 1, k, 0] = f1 + eta * ahead
            buf[m, s + 1, k, 1] = l2 + eta * behind
            trade(m, s + 1, k).start()
        value = jnp.where(right, behind, ahead)
        near[m, k, 0] += add_l * value
        near[m, k, 1] += add_r * value

    @pl.loop(0, nf)
    def _(k):
        trade(0, 0, k).start()

    mh[...], ml[...] = halves(operator[...])
    row = lax.broadcasted_iota(jnp.int32, (height, height), 0).astype(jnp.float32)
    column = lax.broadcasted_iota(jnp.int32, (height, height), 1).astype(jnp.float32)
    down = lax.broadcasted_iota(jnp.int32, (height, 1), 0).astype(jnp.float32)
    along = lax.broadcasted_iota(jnp.int32, (1, height), 1).astype(jnp.float32)

    @pl.loop(0, nf)
    def _(k):
        larger, base, log = diffusive_band(jnp.full((1, height), rates[k], jnp.float32))
        _, _, tall = diffusive_band(jnp.full((height, 1), rates[k], jnp.float32))
        scale = 1.0 / (larger * (1.0 - base * base) * rising(height + 1.0, log))
        upper = rising(down + 1.0, tall) * (rising(height - along, log) * scale)
        lower = rising(height - down, tall) * (rising(along + 1.0, log) * scale)
        green = jnp.exp(jnp.abs(row - column) * log) * jnp.where(row <= column, upper, lower)
        gh[k], gl[k] = halves(green)
        rate = jnp.full((tiles, lane), rates[k], jnp.float32)
        gamma = edge_weights(rate, jnp.zeros((tiles, lane), jnp.float32), height, 0)
        eta = edge_weights(rate, jnp.zeros((tiles, lane), jnp.float32), height, 1)
        for s, cs in enumerate(merge_table(gamma, eta, steps, me)):
            for c in range(5):
                table[1, s, c, k] = cs[c]

    step = 256
    gap = (lax.broadcasted_iota(jnp.int32, (step + 2 * strip, step), 0)
           - lax.broadcasted_iota(jnp.int32, (step + 2 * strip, step), 1) - strip)
    size = jnp.abs(gap)
    taps = jnp.where(size == 1, 45.0, jnp.where(size == 2, -9.0, jnp.where(size == 3, 1.0, 0.0)))
    stencil[...] = jnp.where(gap < 0, -taps, taps).astype(jnp.bfloat16)

    def sweep(p):
        for i in range(len(nexts)):
            side(i, p).wait()
        ph[:, :strip], pq[:, :strip] = halves(strips[0, p])
        ph[:, strip + width :], pq[:, strip + width :] = halves(strips[len(nexts) - 1, p])
        z = p % nz
        for c in range(0, width, step):
            cs = slice(strip + c, strip + c + step)
            ph[:, cs], pq[:, cs] = halves(planes[p, :, c : c + step])
        for c in range(0, width, step):
            cs = slice(c, c + step + 2 * strip)
            sw = (jnp.dot(ph[:, cs], stencil[...], preferred_element_type=jnp.float32)
                  + jnp.dot(pq[:, cs], stencil[...], preferred_element_type=jnp.float32)) * (1.0 / 60.0)
            tend[p, :, c : c + step] = planes[z, :, c : c + step] * sw

    for s in range(steps):
        pl.loop(s * np_ // steps, (s + 1) * np_ // steps)(sweep)
        pl.loop(0, nf)(functools.partial(merge, 0, s))
    speed.wait()
    rows[...] = jnp.zeros(rows.shape, jnp.float32)

    def plane(k, z):
        p = k * nz + z
        for t in range(tiles):
            ts = slice(t * lane, (t + 1) * lane)
            for r in range(2):
                rows[r : r + 1, ts] = halo[2, r, p, t : t + 1, :]
                rows[2 + r : 3 + r, ts] = halo[3, r, p, t : t + 1, :]
                rows[4 + r : 5 + r, ts] = near[0, k, r, z, t : t + 1, :]
        for c in range(0, width, step):
            cs = slice(c, c + step)
            f = planes[p, :, cs]
            fh[:height, cs], fl[:height, cs] = halves(f)
            fh[height:, cs], fl[height:, cs] = halves(rows[:, cs])
            slope = dot3(mh[...], ml[...], fh[:, cs], fl[:, cs])
            t_ = -(tend[p, :, cs] + wv[z, :, cs] * slope)
            tend[p, :, cs] = t_
            rh, rl = halves(2.0 * f + time_step * t_)
            q = dot3(gh[k], gl[k], rh, rl)
            part[p, :, cs] = q - f
            for t in range(step // lane):
                ts = slice(t * lane, (t + 1) * lane)
                at_t = slice(c // lane + t, c // lane + t + 1)
                buf[1, 0, k, 0, z, at_t, :] = q[:1, ts]
                buf[1, 0, k, 1, z, at_t, :] = q[height - 1 :, ts]

    @pl.loop(0, nf)
    def _(k):
        pl.loop(0, nz)(functools.partial(plane, k))
        trade(1, 0, k).start()

    for s in range(steps):
        pl.loop(0, nf)(functools.partial(merge, 1, s))
    beyond[...] = near[1]


def last_kernel(rates, tend, part, near, t_out, a_out, stage, sem):
    np_, height, width = part.shape
    nf = near.shape[0]
    nz = np_ // nf
    first = pltpu.make_async_copy(tend, t_out, sem.at[np_])
    first.start()
    ids = lax.broadcasted_iota(jnp.int32, (height, lane), 0).astype(jnp.float32)

    def put(p):
        return pltpu.make_async_copy(stage.at[p], a_out.at[p], sem.at[p])

    @pl.loop(0, nf)
    def _(k):
        rate = jnp.full((height, lane), rates[k], jnp.float32)
        wl, wr = (edge_weights(rate, ids, height, e) for e in range(2))
        for z in range(nz):
            p = k * nz + z
            for t in range(width // lane):
                ts = slice(t * lane, (t + 1) * lane)
                stage[p, :, ts] = (part[p, :, ts] + wl * near[k, 0, z, t : t + 1, :]
                                   + wr * near[k, 1, z, t : t + 1, :])
            put(p).start()

    @pl.loop(0, np_)
    def _(p):
        put(p).wait()

    first.wait()


def on_device(count, streams, fields, wall_velocity, diffusion):
    nf, nz, height, width = fields.shape
    planes = nf * nz
    tiles = width // lane
    f32 = jnp.float32
    bf16 = jnp.bfloat16
    steps = int(math.log2(count))
    flat = fields.reshape(planes, height, width)
    operator = compact_operator(height)
    extra = 16
    wide = np.zeros((height, height + extra), np.float32)
    wide[:, : height + 6] = operator
    corners = [(float(operator[0, height + 4]), float(operator[0, height + 5]))]
    ends = [[float(operator[j, height + i]) for i in range(4)] for j in (0, height - 1)]
    coef = np.stack([np.repeat(operator[j, :height, None], lane, 1) for j in (0, height - 1)]).astype(np.float32)

    vmem = pl.BlockSpec(memory_space=pltpu.VMEM)
    smem = pl.BlockSpec(memory_space=pltpu.SMEM)
    hbm = pl.BlockSpec(memory_space=pltpu.HBM)
    nrecv = 1 if streams == 2 else 2
    tile = (tiles, lane)
    dma = pltpu.SemaphoreType.DMA
    whole = jax.ShapeDtypeStruct(flat.shape, f32)
    tend, part, beyond = pl.pallas_call(
        functools.partial(big_kernel, count, streams, nf, nz, ends, corners),
        out_shape=(whole, whole, jax.ShapeDtypeStruct((nf, 2, nz) + tile, f32)),
        in_specs=[smem, hbm, hbm, hbm, hbm],
        out_specs=(vmem, vmem, vmem),
        scratch_shapes=[
            pltpu.VMEM(coef.shape, f32),
            pltpu.VMEM(wide.shape, f32),
            pltpu.VMEM((planes, height, width), f32),
            pltpu.VMEM((nz, height, width), f32),
            pltpu.VMEM((2, planes, sub, width), f32),
            pltpu.VMEM((4, 2, planes) + tile, f32),
            pltpu.VMEM((planes, height, lane), f32),
            pltpu.VMEM((nrecv, planes, height, lane), f32),
            pltpu.VMEM((2, steps, nf, 2, nz) + tile, f32),
            pltpu.VMEM((2, steps, nf, 2, nz) + tile, f32),
            pltpu.VMEM((2, nf, 2, nz) + tile, f32),
            pltpu.VMEM((2, steps, 5, nf) + tile, f32),
            pltpu.VMEM((height, height + extra), bf16),
            pltpu.VMEM((height, height + extra), bf16),
            pltpu.VMEM((nf, height, height), bf16),
            pltpu.VMEM((nf, height, height), bf16),
            pltpu.VMEM((extra, width), f32),
            pltpu.VMEM((height, width + 2 * lane), bf16),
            pltpu.VMEM((height, width + 2 * lane), bf16),
            pltpu.VMEM((256 + 2 * lane, 256), bf16),
            pltpu.VMEM((height + extra, width), bf16),
            pltpu.VMEM((height + extra, width), bf16),
            dma((2,)), dma((planes + 2,)), dma, dma((2,)), dma((2,)),
            dma((nrecv, planes)), dma((nrecv, planes)),
            dma((2, steps, nf)), dma((2, steps, nf)),
        ],
        compiler_params=pltpu.CompilerParams(
            collective_id=0, has_side_effects=True, vmem_limit_bytes=36 * 2**20),
    )(diffusion, jnp.asarray(coef), jnp.asarray(wide), flat, wall_velocity)

    tendency, advanced = pl.pallas_call(
        last_kernel,
        out_shape=(whole, whole),
        in_specs=[smem, vmem, vmem, vmem],
        out_specs=(hbm, hbm),
        scratch_shapes=[pltpu.VMEM(flat.shape, f32), dma((planes + 1,))],
        compiler_params=pltpu.CompilerParams(vmem_limit_bytes=16 * 2**20),
    )(diffusion, tend, part, beyond)
    return tendency.reshape(fields.shape), advanced.reshape(fields.shape)


def solution(mesh):
    in_specs = (P(None, None, "wall", "stream"), P(None, "wall", "stream"), P())
    out_specs = (P(None, None, "wall", "stream"), P(None, None, "wall", "stream"))
    body = functools.partial(on_device, mesh.shape["wall"], mesh.shape["stream"])
    return jax.shard_map(body, mesh=mesh, in_specs=in_specs, out_specs=out_specs, check_vma=False)
```
